32 devices in a mesh: tm: 8 (over y, x, core), tile: 4 (over z).
Axes of the slice: x: 2, y: 2, z: 4, core: 2. Of those that a mesh axis runs over, the one named last changes fastest.
Arguments:
- local_inv: bfloat16 [16, 2048, 2048], P('tm', None, 'tile'), as said below
- seed_inv: float32 [8, 2048, 2048], P('tm', None, 'tile'), as said below
- band: float32 [16, 16, 3, 128, 128], P('tm', 'tile'), may hold values from -0.25 to 0.25
- pattern: int32 [16, 16, 3], P('tm', 'tile'), may hold values from 0 to 1, as said below
Outputs:
- sigma_first: float32 [8, 2048, 2048], P('tm', None, 'tile')
- variances: float32 [16, 2048], P('tm', 'tile')
The draws below stay inside these ranges and needn't reach their ends.
Inputs may be any that keep to these rules, and one draw needn't show every extreme that they name: Every entry is 0 or 1; the middle entry pattern[j, b, 1] is 1; pattern[j, 0, 0] and pattern[j, 15, 2] are 0. `local_inv`: each matrix is symmetric. `seed_inv`: each matrix is symmetric.
All inputs are finite; a program needn't handle non-finite values.
Results may differ from the reference program's by a relative error of at most 0.0003.
Values sent between devices are 32-bit elements; how exact they have to be, the bound alone decides.
A program may use at most 128 MiB of HBM per device.

```python
import jax
import jax.numpy as jnp
from jax import lax

TILE_ROWS = 128
BLOCK = 2048
TILES = 16
TBLOCKS = 16
N_TM = 8


def symmetric_field(key, count):
    first = jax.random.fold_in(key, 0)
    third = jax.random.fold_in(key, 2)
    noise = jax.random.normal(first, (count, BLOCK, BLOCK), jnp.float32)
    field = 0.35 * (noise + jnp.swapaxes(noise, 1, 2))
    lift = 1.5 + jax.random.uniform(third, (count, BLOCK), jnp.float32)
    return field + jnp.eye(BLOCK, dtype=jnp.float32)[None] * lift[:, :, None]


def draw_local_inv(key, part):
    return symmetric_field(jax.random.fold_in(key, 11), TBLOCKS).astype(jnp.bfloat16)


def draw_seed_inv(key, part):
    return symmetric_field(jax.random.fold_in(key, 23), N_TM)


def draw_pattern(key, part):
    coins = jax.random.randint(jax.random.fold_in(key, 37), (TBLOCKS, TILES, 3), 0, 4)
    filled = jnp.where(coins > 0, 1, 0)
    column = jnp.arange(3)[None, None, :]
    tile_index = jnp.arange(TILES)[None, :, None]
    filled = jnp.where(column == 1, 1, filled)
    filled = jnp.where((tile_index == 0) & (column == 0), 0, filled)
    filled = jnp.where((tile_index == TILES - 1) & (column == 2), 0, filled)
    return filled.astype(jnp.int32)


def shard_levels(key, dims, pieces, low, largest):
    factor_of = 1.0
    for dim, parts in pieces:
        steps = jax.random.uniform(jax.random.fold_in(jax.random.fold_in(key, 6), dim), (parts,), jnp.float32, low / len(pieces), largest / len(pieces))
        factor_of = factor_of * jnp.repeat(jnp.exp(steps), dims[dim] // parts).reshape((-1,) + (1,) * (len(dims) - 1 - dim))
    return factor_of


def gaussian(stream_key, dims, deviation, reach, cuts=(), held_as=jnp.bfloat16):
    values = deviation * jax.random.normal(stream_key, dims, jnp.float32)
    if cuts:
        values = values * shard_levels(stream_key, dims, cuts, -0.22, 0.18)
    return jnp.clip(values, -reach, reach).astype(held_as)


def setup_inputs(seed: int = 0) -> dict:
    key_of = jax.random.split(jax.random.key(seed), 5)
    return {
        "local_inv": draw_local_inv(jax.random.fold_in(key_of[4], 71), 0),
        "seed_inv": draw_seed_inv(jax.random.fold_in(key_of[4], 71), 0),
        "band": gaussian(key_of[2], (TBLOCKS, TILES, 3, TILE_ROWS, TILE_ROWS), (4 * TILE_ROWS) ** -0.5, 0.25, ((0, 8), (1, 4)), jnp.float32),
        "pattern": draw_pattern(jax.random.fold_in(key_of[4], 71), 0),
    }


HIGH = lax.Precision.HIGHEST


def right_apply(field, weff):
    tiles = weff.shape[0]
    tile_rows = weff.shape[2]
    count = field.shape[0]
    spread = field.reshape(count, tiles, tile_rows)
    padded = jnp.pad(spread, ((0, 0), (1, 1), (0, 0)))
    windows = jnp.stack([padded[:, offset:offset + tiles] for offset in range(3)], axis=2)
    product = jnp.einsum('rbkc,bkcd->rbd', windows, weff, precision=HIGH)
    return product.reshape(count, count)


def left_apply(product, weff):
    tiles = weff.shape[0]
    tile_rows = weff.shape[2]
    count = product.shape[1]
    spread = product.reshape(tiles, tile_rows, count)
    padded = jnp.pad(spread, ((1, 1), (0, 0), (0, 0)))
    windows = jnp.stack([padded[offset:offset + tiles] for offset in range(3)], axis=1)
    result = jnp.einsum('skcd,skce->sde', weff, windows, precision=HIGH)
    return result.reshape(tiles * tile_rows, count)


def reference(local_inv, seed_inv, band, pattern):
    weff = band * pattern.astype(jnp.float32)[..., None, None]
    count = local_inv.shape[1]
    nexts = jnp.concatenate([seed_inv[1:], jnp.zeros_like(seed_inv[:1])], axis=0)
    pairs = local_inv.reshape(N_TM, 2, count, count)
    wpairs = weff.reshape((N_TM, 2) + weff.shape[1:])

    def one_part(items):
        local_pair, w_pair, next_field = items
        sigma_odd = local_pair[1].astype(jnp.float32) + left_apply(right_apply(next_field, w_pair[1]), w_pair[1])
        sigma_even = local_pair[0].astype(jnp.float32) + left_apply(right_apply(sigma_odd, w_pair[0]), w_pair[0])
        return sigma_even, jnp.stack([jnp.diagonal(sigma_even), jnp.diagonal(sigma_odd)])

    sigma_first, diagonals = lax.map(one_part, (pairs, wpairs, nexts))
    variances = diagonals.reshape(2 * N_TM, count)
    return sigma_first, variances
```

```python
import functools

import jax
import jax.numpy as jnp
from jax import lax
from jax.experimental import pallas as pl
from jax.experimental.pallas import tpu as pltpu
from jax.sharding import PartitionSpec as P

F32 = jnp.float32
BF16 = jnp.bfloat16
MESH = pl.DeviceIdType.MESH


def split(value):
    high = value.astype(BF16)
    return high, (value - high.astype(F32)).astype(BF16)


def dot(a, b):
    return lax.dot_general(a, b, (((1,), (0,)), ((), ())), preferred_element_type=F32)


def split_dot(a_high, a_low, b_high, b_low):
    return dot(a_high, b_high) + (dot(a_high, b_low) + dot(a_low, b_high))


def kernel(parts, ranks, local_ref, seed_ref, weff_ref, out_ref, var_ref,
           nxt, odd, wbuf, m_high, m_low, loc, wc_high, wc_low, wt_high, wt_low,
           wsend, wrecv, nsend, nrecv, hsend, hrecv, lsem):
    p, t = lax.axis_index("tm"), lax.axis_index("tile")
    rows, width = seed_ref.shape[1], seed_ref.shape[2]
    tiles, tr = wbuf.shape[1], wbuf.shape[3]
    lt = width // tr
    g = 2 if lt % 2 == 0 else 1
    span = (g + 2) * tr
    inner = pl.ds(tr, width)
    left_halo, right_halo = pl.ds(0, tr), pl.ds(tr + width, tr)
    has_right, has_left = t < ranks - 1, t > 0
    has_next = p < parts - 1

    barrier = pltpu.get_barrier_semaphore()
    around = [(a, b) for a in (-1, 0, 1) for b in (-1, 0, 1) if (a, b) != (0, 0)]

    def present(a, b):
        return (p + a >= 0) & (p + a < parts) & (t + b >= 0) & (t + b < ranks)

    for a, b in around:
        @pl.when(present(a, b))
        def _(a=a, b=b):
            pl.semaphore_signal(barrier, inc=1, device_id={"tm": p + a, "tile": t + b}, device_id_type=MESH)
    near_tm = 1 + jnp.where(p > 0, 1, 0) + jnp.where(p < parts - 1, 1, 0)
    near_tile = 1 + jnp.where(t > 0, 1, 0) + jnp.where(t < ranks - 1, 1, 0)
    pl.semaphore_wait(barrier, near_tm * near_tile - 1)

    def toward(d):
        return (1, has_right) if d == 0 else (-1, has_left)

    def own_w(j, d):
        step, _ = toward(d)
        return pltpu.make_async_remote_copy(
            src_ref=weff_ref.at[j], dst_ref=wbuf.at[j, pl.ds(t * lt, lt)],
            send_sem=wsend.at[j, d, 0], recv_sem=wrecv.at[j, d, 1],
            device_id={"tile": t + step}, device_id_type=MESH)

    def relay_w(j, d, k):
        step, _ = toward(d)
        part = wbuf.at[j, pl.ds((t - step * k) * lt, lt)]
        return pltpu.make_async_remote_copy(
            src_ref=part, dst_ref=part,
            send_sem=wsend.at[j, d, k], recv_sem=wrecv.at[j, d, k + 1],
            device_id={"tile": t + step}, device_id_type=MESH)

    def arriving_w(j, d, k):
        step, _ = toward(d)
        part = wbuf.at[j, pl.ds((t - step * k) * lt, lt)]
        return pltpu.make_async_remote_copy(
            src_ref=part, dst_ref=part,
            send_sem=wsend.at[j, d, k], recv_sem=wrecv.at[j, d, k],
            device_id={"tile": t - step}, device_id_type=MESH)

    def comes(d, k):
        return t - k >= 0 if d == 0 else t + k < ranks

    def start_own(j):
        for d in (1, 0):
            @pl.when(toward(d)[1])
            def _(d=d):
                own_w(j, d).start()

    def receive(j, k):
        for d in (1, 0):
            @pl.when(comes(d, k))
            def _(d=d):
                arriving_w(j, d, k).wait_recv()

                @pl.when(toward(d)[1])
                def _():
                    relay_w(j, d, k).start()

    def seed_copy(index):
        if index == 0:
            src, dst, target = seed_ref.at[0], nxt.at[:, inner], t
        elif index == 1:
            src, dst, target = seed_ref.at[0, :, pl.ds(width - tr, tr)], nxt.at[:, left_halo], t + 1
        else:
            src, dst, target = seed_ref.at[0, :, pl.ds(0, tr)], nxt.at[:, right_halo], t - 1
        return pltpu.make_async_remote_copy(
            src_ref=src, dst_ref=dst, send_sem=nsend.at[index], recv_sem=nrecv.at[index],
            device_id={"tm": p - 1, "tile": target}, device_id_type=MESH)

    seed_sent = ((0, p > 0), (1, (p > 0) & has_right), (2, (p > 0) & has_left))
    seed_received = ((0, has_next), (1, has_next & has_left), (2, has_next & has_right))

    def halo_copy(d):
        if d == 0:
            src, dst, target = odd.at[:, pl.ds(width, tr)], odd.at[:, left_halo], t + 1
        else:
            src, dst, target = odd.at[:, pl.ds(tr, tr)], odd.at[:, right_halo], t - 1
        return pltpu.make_async_remote_copy(
            src_ref=src, dst_ref=dst, send_sem=hsend.at[d], recv_sem=hrecv.at[d],
            device_id={"tile": target}, device_id_type=MESH)

    start_own(1)
    for index, does in seed_sent:
        @pl.when(does)
        def _(index=index):
            seed_copy(index).start()
    own_local = [pltpu.make_async_copy(weff_ref.at[j], wbuf.at[j, pl.ds(t * lt, lt)], lsem.at[j]) for j in (0, 1)]
    locals_in = pltpu.make_async_copy(local_ref, loc, lsem.at[2])
    for copy in own_local + [locals_in]:
        copy.start()

    zero_halo = jnp.zeros((rows, tr), F32)
    for missing, place in ((t == 0, left_halo), (t == ranks - 1, right_halo)):
        @pl.when(missing)
        def _(place=place):
            odd[:, place] = zero_halo

            @pl.when(has_next)
            def _():
                nxt[:, place] = zero_halo

    @pl.when(p == parts - 1)
    def _():
        nxt[...] = jnp.zeros_like(nxt)

    for ref in (m_high, m_low):
        ref[pl.ds(0, tr), :] = jnp.zeros((tr, width), BF16)
        ref[pl.ds(tr + rows, tr), :] = jnp.zeros((tr, width), BF16)
    for ref in (wc_high, wc_low, wt_high, wt_low):
        ref[...] = jnp.zeros_like(ref)
    for copy in own_local:
        copy.wait()

    chunk = 256

    def column_product(field, j):
        for i in range(lt // g):
            for c in range(g):
                for k in range(3):
                    high, low = split(wbuf[j, t * lt + i * g + c, k])
                    at = (i, pl.ds((c + k) * tr, tr), pl.ds(c * tr, tr))
                    wc_high[at] = high
                    wc_low[at] = low

        @pl.loop(0, rows // chunk)
        def _(r):
            start = pl.multiple_of(r * chunk, chunk)
            for i in range(lt // g):
                high, low = split(field[pl.ds(start, chunk), pl.ds(i * g * tr, span)])
                value = split_dot(high, low, wc_high[i], wc_low[i])
                at = (pl.ds(pl.multiple_of(start + tr, tr), chunk), pl.ds(i * g * tr, g * tr))
                high, low = split(value)
                m_high[at] = high
                m_low[at] = low

    def left_rows(j, owner, target, columns):
        @pl.loop(0, lt // g)
        def _(i):
            first = owner * lt + i * g
            for c in range(g):
                for k in range(3):
                    high, low = split(wbuf[j, first + c, k].T)
                    at = (pl.ds(c * tr, tr), pl.ds((c + k) * tr, tr))
                    wt_high[at] = high
                    wt_low[at] = low
            start = pl.multiple_of(first * tr, tr)
            source = pl.ds(start, span)
            value = split_dot(wt_high[...], wt_low[...], m_high[source, :], m_low[source, :])
            place = pl.ds(start, g * tr)
            target[place, columns] = loc[j, place, :].astype(F32) + value

    def left_round(j, k, target, columns):
        for d in (1, 0):
            @pl.when(comes(d, k))
            def _(d=d):
                left_rows(j, t - k if d == 0 else t + k, target, columns)

    def diagonal(index, field, offset):
        eye = lax.broadcasted_iota(jnp.int32, (tr, tr), 0) == lax.broadcasted_iota(jnp.int32, (tr, tr), 1)
        for c in range(lt):
            tile = field[pl.ds(pl.multiple_of(t * width + c * tr, tr), tr), pl.ds(offset + c * tr, tr)]
            var_ref[pl.ds(index, 1), pl.ds(c * tr, tr)] = jnp.sum(jnp.where(eye, tile, 0.0), axis=0, keepdims=True)

    receive(1, 1)
    start_own(0)
    for index, does in seed_received:
        @pl.when(does)
        def _(index=index):
            seed_copy(index).wait_recv()
    column_product(nxt, 1)
    locals_in.wait()
    left_rows(1, t, odd, inner)
    left_round(1, 1, odd, inner)

    @pl.loop(2, ranks)
    def _(k):
        receive(1, k)
        left_round(1, k, odd, inner)

    diagonal(1, odd, tr)
    for d, does in ((1, has_left), (0, has_right)):
        @pl.when(does)
        def _(d=d):
            halo_copy(d).start()

    @pl.loop(1, ranks - 1)
    def _(k):
        receive(0, k)

    for d, does in ((0, has_left), (1, has_right)):
        @pl.when(does)
        def _(d=d):
            halo_copy(d).wait_recv()
    column_product(odd, 0)
    everything = pl.ds(0, width)
    left_rows(0, t, out_ref, everything)

    @pl.loop(1, ranks - 1)
    def _(k):
        left_round(0, k, out_ref, everything)

    receive(0, ranks - 1)
    left_round(0, ranks - 1, out_ref, everything)
    diagonal(0, out_ref, 0)

    for j in (1, 0):
        for d in (1, 0):
            @pl.when(toward(d)[1])
            def _(j=j, d=d):
                own_w(j, d).wait_send()

                @pl.loop(1, ranks - 1)
                def _(k):
                    @pl.when(comes(d, k))
                    def _():
                        relay_w(j, d, k).wait_send()
    for index, does in seed_sent:
        @pl.when(does)
        def _(index=index):
            seed_copy(index).wait_send()
    for d, does in ((0, has_right), (1, has_left)):
        @pl.when(does)
        def _(d=d):
            halo_copy(d).wait_send()


def per_device(parts, ranks, local_inv, seed_inv, band, pattern):
    weff = band * pattern.astype(F32)[..., None, None]
    rows, width = seed_inv.shape[1:]
    lt, tr = band.shape[1], band.shape[3]
    tiles = rows // tr
    g = 2 if lt % 2 == 0 else 1
    span = (g + 2) * tr
    dma = pltpu.SemaphoreType.DMA
    out, var = pl.pallas_call(
        functools.partial(kernel, parts, ranks),
        out_shape=(jax.ShapeDtypeStruct((rows, width), F32), jax.ShapeDtypeStruct((2, width), F32)),
        in_specs=[pl.BlockSpec(memory_space=pl.ANY)] * 3,
        out_specs=(pl.BlockSpec(memory_space=pltpu.VMEM), pl.BlockSpec(memory_space=pltpu.VMEM)),
        scratch_shapes=[
            pltpu.VMEM((rows, width + 2 * tr), F32),
            pltpu.VMEM((rows, width + 2 * tr), F32),
            pltpu.VMEM((2, tiles, 3, tr, tr), F32),
            pltpu.VMEM((rows + 2 * tr, width), BF16),
            pltpu.VMEM((rows + 2 * tr, width), BF16),
            pltpu.VMEM((2, rows, width), BF16),
            pltpu.VMEM((lt // g, span, g * tr), BF16),
            pltpu.VMEM((lt // g, span, g * tr), BF16),
            pltpu.VMEM((g * tr, span), BF16),
            pltpu.VMEM((g * tr, span), BF16),
            dma((2, 2, ranks + 1)),
            dma((2, 2, ranks + 1)),
            dma((3,)),
            dma((3,)),
            dma((2,)),
            dma((2,)),
            dma((3,)),
        ],
        compiler_params=pltpu.CompilerParams(
            collective_id=0, has_side_effects=True, vmem_limit_bytes=60 * 1024 * 1024
        ),
    )(local_inv, seed_inv, weff)
    return out[None], var


def solution(mesh):
    placed = (
        P("tm", None, "tile"),
        P("tm", None, "tile"),
        P("tm", "tile", None, None, None),
        P("tm", "tile", None),
    )
    return jax.shard_map(
        functools.partial(per_device, mesh.shape["tm"], mesh.shape["tile"]),
        mesh=mesh,
        in_specs=placed,
        out_specs=(P("tm", None, "tile"), P("tm", "tile")),
        check_vma=False,
    )
```

```python
import functools

import jax
import jax.numpy as jnp
from jax import lax
from jax.experimental import pallas as pl
from jax.experimental.pallas import tpu as pltpu
from jax.sharding import PartitionSpec as P

F32 = jnp.float32
BF16 = jnp.bfloat16
MESH = pl.DeviceIdType.MESH


def split(value):
    high = value.astype(BF16)
    return high, (value - high.astype(F32)).astype(BF16)


def dot(a, b):
    return lax.dot_general(a, b, (((1,), (0,)), ((), ())), preferred_element_type=F32)


def split_dot(a_high, a_low, b_high, b_low):
    return dot(a_high, b_high) + (dot(a_high, b_low) + dot(a_low, b_high))


def kernel(parts, ranks, local_ref, seed_ref, band_ref, pattern_ref, out_ref, var_ref,
           nxt, odd, wbuf, m_high, m_low, loc, wc_high, wc_low, wt_high, wt_low,
           wsend, wrecv, nsend, nrecv, hsend, hrecv, lsem):
    p, t = lax.axis_index("tm"), lax.axis_index("tile")
    rows, width = seed_ref.shape[1], seed_ref.shape[2]
    tiles, tr = wbuf.shape[1], wbuf.shape[3]
    lt = width // tr
    g = 2 if lt % 2 == 0 else 1
    span = (g + 2) * tr
    inner = pl.ds(tr, width)
    left_halo, right_halo = pl.ds(0, tr), pl.ds(tr + width, tr)
    has_right, has_left = t < ranks - 1, t > 0
    has_next = p < parts - 1

    barrier = pltpu.get_barrier_semaphore()
    around = [(a, b) for a in (-1, 0, 1) for b in (-1, 0, 1) if (a, b) != (0, 0)]

    def present(a, b):
        return (p + a >= 0) & (p + a < parts) & (t + b >= 0) & (t + b < ranks)

    for a, b in around:
        @pl.when(present(a, b))
        def _(a=a, b=b):
            pl.semaphore_signal(barrier, inc=1, device_id={"tm": p + a, "tile": t + b}, device_id_type=MESH)
    near_tm = 1 + jnp.where(p > 0, 1, 0) + jnp.where(p < parts - 1, 1, 0)
    near_tile = 1 + jnp.where(t > 0, 1, 0) + jnp.where(t < ranks - 1, 1, 0)
    pl.semaphore_wait(barrier, near_tm * near_tile - 1)

    def toward(d):
        return (1, has_right) if d == 0 else (-1, has_left)

    def relay_w(j, d, k):
        step, _ = toward(d)
        part = wbuf.at[j, pl.ds((t - step * k) * lt, lt)]
        return pltpu.make_async_remote_copy(
            src_ref=part, dst_ref=part,
            send_sem=wsend.at[j, d, k], recv_sem=wrecv.at[j, d, k + 1],
            device_id={"tile": t + step}, device_id_type=MESH)

    def arriving_w(j, d, k):
        step, _ = toward(d)
        part = wbuf.at[j, pl.ds((t - step * k) * lt, lt)]
        return pltpu.make_async_remote_copy(
            src_ref=part, dst_ref=part,
            send_sem=wsend.at[j, d, k], recv_sem=wrecv.at[j, d, k],
            device_id={"tile": t - step}, device_id_type=MESH)

    def comes(d, k):
        return t - k >= 0 if d == 0 else t + k < ranks

    def start_own(j):
        for d in (1, 0):
            @pl.when(toward(d)[1])
            def _(d=d):
                relay_w(j, d, 0).start()

    def receive(j, k):
        for d in (1, 0):
            @pl.when(comes(d, k))
            def _(d=d):
                arriving_w(j, d, k).wait_recv()

                @pl.when(toward(d)[1])
                def _():
                    relay_w(j, d, k).start()

    def block(u):
        return pl.ds(u * width, width)

    def seed_copy(index, u):
        if index == 0:
            src, dst, target = seed_ref.at[0], nxt.at[:, inner], t
        elif index == 1:
            src, dst, target = seed_ref.at[0, block(u), pl.ds(width - tr, tr)], nxt.at[block(u), left_halo], t + 1
        else:
            src, dst, target = seed_ref.at[0, block(u), pl.ds(0, tr)], nxt.at[block(u), right_halo], t - 1
        return pltpu.make_async_remote_copy(
            src_ref=src, dst_ref=dst, send_sem=nsend.at[index, u], recv_sem=nrecv.at[index, u],
            device_id={"tm": p - 1, "tile": target}, device_id_type=MESH)

    def halo_copy(d, u):
        if d == 0:
            src, dst, target = odd.at[block(u), pl.ds(width, tr)], odd.at[block(u), left_halo], t + 1
        else:
            src, dst, target = odd.at[block(u), pl.ds(tr, tr)], odd.at[block(u), right_halo], t - 1
        return pltpu.make_async_remote_copy(
            src_ref=src, dst_ref=dst, send_sem=hsend.at[d, u], recv_sem=hrecv.at[d, u],
            device_id={"tile": target}, device_id_type=MESH)

    def blocks_but(skipped, does, action):
        @pl.loop(0, ranks)
        def _(u):
            @pl.when(does & (u != skipped))
            def _():
                action(u)

    def mirror(field):
        for does, row, place in ((has_left, t * width - tr, left_halo), (has_right, (t + 1) * width, right_halo)):
            @pl.when(does)
            def _(row=row, place=place):
                for i in range(lt):
                    tile = field[pl.ds(pl.multiple_of(row, tr), tr), pl.ds(tr + i * tr, tr)]
                    field[pl.ds(pl.multiple_of(t * width + i * tr, tr), tr), place] = tile.T

    own_local = [pltpu.make_async_copy(band_ref.at[j], wbuf.at[j, pl.ds(t * lt, lt)], lsem.at[j]) for j in (0, 1)]
    locals_in = pltpu.make_async_copy(local_ref, loc, lsem.at[2])
    for copy in own_local[::-1]:
        copy.start()
    blocks_but(t + 1, (p > 0) & has_right, lambda u: seed_copy(1, u).start())
    blocks_but(t - 1, (p > 0) & has_left, lambda u: seed_copy(2, u).start())

    @pl.when(p > 0)
    def _():
        seed_copy(0, 0).start()

    locals_in.start()
    for j in (1, 0):
        own_local[j].wait()
        for b in range(lt):
            for k in range(3):
                at = (j, t * lt + b, k)
                wbuf[at] = wbuf[at] * pattern_ref[j, b, k].astype(F32)

    zero_halo = jnp.zeros((rows, tr), F32)
    for missing, place in ((t == 0, left_halo), (t == ranks - 1, right_halo)):
        @pl.when(missing)
        def _(place=place):
            odd[:, place] = zero_halo

            @pl.when(has_next)
            def _():
                nxt[:, place] = zero_halo

    @pl.when(p == parts - 1)
    def _():
        nxt[...] = jnp.zeros_like(nxt)

    for ref in (m_high, m_low):
        ref[pl.ds(0, tr), :] = jnp.zeros((tr, width), BF16)
        ref[pl.ds(tr + rows, tr), :] = jnp.zeros((tr, width), BF16)
    for ref in (wc_high, wc_low, wt_high, wt_low):
        ref[...] = jnp.zeros_like(ref)
    start_own(1)
    start_own(0)

    chunk = 256

    def column_product(field, j):
        for i in range(lt // g):
            for c in range(g):
                for k in range(3):
                    high, low = split(wbuf[j, t * lt + i * g + c, k])
                    at = (i, pl.ds((c + k) * tr, tr), pl.ds(c * tr, tr))
                    wc_high[at] = high
                    wc_low[at] = low

        @pl.loop(0, rows // chunk)
        def _(r):
            start = pl.multiple_of(r * chunk, chunk)
            for i in range(lt // g):
                high, low = split(field[pl.ds(start, chunk), pl.ds(i * g * tr, span)])
                value = split_dot(high, low, wc_high[i], wc_low[i])
                at = (pl.ds(pl.multiple_of(start + tr, tr), chunk), pl.ds(i * g * tr, g * tr))
                high, low = split(value)
                m_high[at] = high
                m_low[at] = low

    def left_rows(j, owner, target, columns):
        @pl.loop(0, lt // g)
        def _(i):
            first = owner * lt + i * g
            for c in range(g):
                for k in range(3):
                    high, low = split(wbuf[j, first + c, k].T)
                    at = (pl.ds(c * tr, tr), pl.ds((c + k) * tr, tr))
                    wt_high[at] = high
                    wt_low[at] = low
            start = pl.multiple_of(first * tr, tr)
            source = pl.ds(start, span)
            value = split_dot(wt_high[...], wt_low[...], m_high[source, :], m_low[source, :])
            place = pl.ds(start, g * tr)
            target[place, columns] = loc[j, place, :].astype(F32) + value

    def left_round(j, k, target, columns):
        for d in (1, 0):
            @pl.when(comes(d, k))
            def _(d=d):
                left_rows(j, t - k if d == 0 else t + k, target, columns)

    def diagonal(index, field, offset):
        eye = lax.broadcasted_iota(jnp.int32, (tr, tr), 0) == lax.broadcasted_iota(jnp.int32, (tr, tr), 1)
        for c in range(lt):
            tile = field[pl.ds(pl.multiple_of(t * width + c * tr, tr), tr), pl.ds(offset + c * tr, tr)]
            var_ref[pl.ds(index, 1), pl.ds(c * tr, tr)] = jnp.sum(jnp.where(eye, tile, 0.0), axis=0, keepdims=True)

    receive(1, 1)

    @pl.when(has_next)
    def _():
        seed_copy(0, 0).wait_recv()

    blocks_but(t, has_next & has_left, lambda u: seed_copy(1, u).wait_recv())
    blocks_but(t, has_next & has_right, lambda u: seed_copy(2, u).wait_recv())
    mirror(nxt)
    column_product(nxt, 1)
    locals_in.wait()
    left_rows(1, t, odd, inner)
    left_round(1, 1, odd, inner)

    @pl.loop(2, ranks)
    def _(k):
        receive(1, k)
        left_round(1, k, odd, inner)

    diagonal(1, odd, tr)
    mirror(odd)
    blocks_but(t - 1, has_left, lambda u: halo_copy(1, u).start())
    blocks_but(t + 1, has_right, lambda u: halo_copy(0, u).start())

    @pl.loop(1, ranks - 1)
    def _(k):
        receive(0, k)

    blocks_but(t, has_left, lambda u: halo_copy(0, u).wait_recv())
    blocks_but(t, has_right, lambda u: halo_copy(1, u).wait_recv())
    column_product(odd, 0)
    everything = pl.ds(0, width)
    left_rows(0, t, out_ref, everything)

    @pl.loop(1, ranks - 1)
    def _(k):
        left_round(0, k, out_ref, everything)

    receive(0, ranks - 1)
    left_round(0, ranks - 1, out_ref, everything)
    diagonal(0, out_ref, 0)

    for j in (1, 0):
        for d in (1, 0):
            @pl.when(toward(d)[1])
            def _(j=j, d=d):
                relay_w(j, d, 0).wait_send()

                @pl.loop(1, ranks - 1)
                def _(k):
                    @pl.when(comes(d, k))
                    def _():
                        relay_w(j, d, k).wait_send()
    @pl.when(p > 0)
    def _():
        seed_copy(0, 0).wait_send()

    blocks_but(t + 1, (p > 0) & has_right, lambda u: seed_copy(1, u).wait_send())
    blocks_but(t - 1, (p > 0) & has_left, lambda u: seed_copy(2, u).wait_send())
    blocks_but(t + 1, has_right, lambda u: halo_copy(0, u).wait_send())
    blocks_but(t - 1, has_left, lambda u: halo_copy(1, u).wait_send())


def per_device(parts, ranks, local_inv, seed_inv, band, pattern):
    rows, width = seed_inv.shape[1:]
    lt, tr = band.shape[1], band.shape[3]
    tiles = rows // tr
    g = 2 if lt % 2 == 0 else 1
    span = (g + 2) * tr
    dma = pltpu.SemaphoreType.DMA
    out, var = pl.pallas_call(
        functools.partial(kernel, parts, ranks),
        out_shape=(jax.ShapeDtypeStruct((rows, width), F32), jax.ShapeDtypeStruct((2, width), F32)),
        in_specs=[pl.BlockSpec(memory_space=pltpu.HBM)] * 3 + [pl.BlockSpec(memory_space=pltpu.SMEM)],
        out_specs=(pl.BlockSpec(memory_space=pltpu.VMEM), pl.BlockSpec(memory_space=pltpu.VMEM)),
        scratch_shapes=[
            pltpu.VMEM((rows, width + 2 * tr), F32),
            pltpu.VMEM((rows, width + 2 * tr), F32),
            pltpu.VMEM((2, tiles, 3, tr, tr), F32),
            pltpu.VMEM((rows + 2 * tr, width), BF16),
            pltpu.VMEM((rows + 2 * tr, width), BF16),
            pltpu.VMEM((2, rows, width), BF16),
            pltpu.VMEM((lt // g, span, g * tr), BF16),
            pltpu.VMEM((lt // g, span, g * tr), BF16),
            pltpu.VMEM((g * tr, span), BF16),
            pltpu.VMEM((g * tr, span), BF16),
            dma((2, 2, ranks + 1)),
            dma((2, 2, ranks + 1)),
            dma((3, ranks)),
            dma((3, ranks)),
            dma((2, ranks)),
            dma((2, ranks)),
            dma((3,)),
        ],
        compiler_params=pltpu.CompilerParams(
            collective_id=0, has_side_effects=True, vmem_limit_bytes=36 * 1024 * 1024
        ),
    )(local_inv, seed_inv, band, pattern)
    return out[None], var


def solution(mesh):
    placed = (
        P("tm", None, "tile"),
        P("tm", None, "tile"),
        P("tm", "tile", None, None, None),
        P("tm", "tile", None),
    )
    return jax.shard_map(
        functools.partial(per_device, mesh.shape["tm"], mesh.shape["tile"]),
        mesh=mesh,
        in_specs=placed,
        out_specs=(P("tm", None, "tile"), P("tm", "tile")),
        check_vma=False,
    )
```

```python
import functools

import jax
import jax.numpy as jnp
from jax import lax
from jax.experimental import pallas as pl
from jax.experimental.pallas import tpu as pltpu
from jax.sharding import PartitionSpec as P

F32 = jnp.float32
BF16 = jnp.bfloat16
MESH = pl.DeviceIdType.MESH


def split(value):
    high = value.astype(BF16)
    return high, (value - high.astype(F32)).astype(BF16)


def dot(a, b):
    return lax.dot_general(a, b, (((1,), (0,)), ((), ())), preferred_element_type=F32)


def split_dot(a_high, a_low, b_high, b_low):
    return dot(a_high, b_high) + (dot(a_high, b_low) + dot(a_low, b_high))


def kernel(parts, ranks, local_ref, seed_ref, band_ref, pattern_ref, out_ref, var_ref,
           nxt, odd, wbuf, m_high, m_low, loc, wc_high, wc_low, wt_high, wt_low,
           wsend, wrecv, nsend, nrecv, hsend, hrecv, lsem):
    p, t = lax.axis_index("tm"), lax.axis_index("tile")
    rows, width = seed_ref.shape[1], seed_ref.shape[2]
    tiles, tr = wbuf.shape[1] // 3, wbuf.shape[3]
    lt = width // tr
    g = 2 if lt % 2 == 0 else 1
    span = (g + 2) * tr
    inner = pl.ds(tr, width)
    left_halo, right_halo = pl.ds(0, tr), pl.ds(tr + width, tr)
    has_right, has_left = t < ranks - 1, t > 0
    has_next = p < parts - 1

    barrier = pltpu.get_barrier_semaphore()
    around = [(a, b) for a in (-1, 0, 1) for b in (-1, 0, 1) if (a, b) != (0, 0)]

    def present(a, b):
        return (p + a >= 0) & (p + a < parts) & (t + b >= 0) & (t + b < ranks)

    for a, b in around:
        @pl.when(present(a, b))
        def _(a=a, b=b):
            pl.semaphore_signal(barrier, inc=1, device_id={"tm": p + a, "tile": t + b}, device_id_type=MESH)
    near_tm = 1 + jnp.where(p > 0, 1, 0) + jnp.where(p < parts - 1, 1, 0)
    near_tile = 1 + jnp.where(t > 0, 1, 0) + jnp.where(t < ranks - 1, 1, 0)
    pl.semaphore_wait(barrier, near_tm * near_tile - 1)

    def toward(d):
        return (1, has_right) if d == 0 else (-1, has_left)

    def with_w(j, d, k, incoming, action):
        step, _ = toward(d)
        owner = t - step * k
        at_end = owner == (0 if d == 0 else ranks - 1)
        for condition, skip in ((at_end, 1), (jnp.logical_not(at_end), 0)):
            @pl.when(condition)
            def _(skip=skip):
                part = wbuf.at[j, pl.ds(owner * lt * 3 + (skip if d == 0 else 0), lt * 3 - skip)]
                action(pltpu.make_async_remote_copy(
                    src_ref=part, dst_ref=part,
                    send_sem=wsend.at[j, d, k], recv_sem=wrecv.at[j, d, k if incoming else k + 1],
                    device_id={"tile": t - step if incoming else t + step}, device_id_type=MESH))

    def comes(d, k):
        return t - k >= 0 if d == 0 else t + k < ranks

    def start_own(j):
        for d in (1, 0):
            @pl.when(toward(d)[1])
            def _(d=d):
                with_w(j, d, 0, False, lambda copy: copy.start())

    def receive(j, k):
        for d in (1, 0):
            @pl.when(comes(d, k))
            def _(d=d):
                with_w(j, d, k, True, lambda copy: copy.wait_recv())

                @pl.when(toward(d)[1])
                def _():
                    with_w(j, d, k, False, lambda copy: copy.start())

    def block(u):
        return pl.ds(u * width, width)

    def seed_copy(index, u):
        if index == 0:
            src, dst, target = seed_ref.at[0], nxt.at[:, inner], t
        elif index == 1:
            src, dst, target = seed_ref.at[0, block(u), pl.ds(width - tr, tr)], nxt.at[block(u), left_halo], t + 1
        else:
            src, dst, target = seed_ref.at[0, block(u), pl.ds(0, tr)], nxt.at[block(u), right_halo], t - 1
        return pltpu.make_async_remote_copy(
            src_ref=src, dst_ref=dst, send_sem=nsend.at[index, u], recv_sem=nrecv.at[index, u],
            device_id={"tm": p - 1, "tile": target}, device_id_type=MESH)

    def halo_copy(d, u):
        if d == 0:
            src, dst, target = odd.at[block(u), pl.ds(width, tr)], odd.at[block(u), left_halo], t + 1
        else:
            src, dst, target = odd.at[block(u), pl.ds(tr, tr)], odd.at[block(u), right_halo], t - 1
        return pltpu.make_async_remote_copy(
            src_ref=src, dst_ref=dst, send_sem=hsend.at[d, u], recv_sem=hrecv.at[d, u],
            device_id={"tile": target}, device_id_type=MESH)

    def blocks_but(skipped, does, action):
        @pl.loop(0, ranks)
        def _(u):
            @pl.when(does & (u != skipped))
            def _():
                action(u)

    def mirror(field):
        for does, row, place in ((has_left, t * width - tr, left_halo), (has_right, (t + 1) * width, right_halo)):
            @pl.when(does)
            def _(row=row, place=place):
                for i in range(lt):
                    tile = field[pl.ds(pl.multiple_of(row, tr), tr), pl.ds(tr + i * tr, tr)]
                    field[pl.ds(pl.multiple_of(t * width + i * tr, tr), tr), place] = tile.T

    own_local = [pltpu.make_async_copy(band_ref.at[j], wbuf.at[j, pl.ds(t * lt * 3, lt * 3)], lsem.at[j]) for j in (0, 1)]
    locals_in = pltpu.make_async_copy(local_ref, loc, lsem.at[2])
    for copy in own_local[::-1]:
        copy.start()
    blocks_but(t + 1, (p > 0) & has_right, lambda u: seed_copy(1, u).start())
    blocks_but(t - 1, (p > 0) & has_left, lambda u: seed_copy(2, u).start())

    @pl.when(p > 0)
    def _():
        seed_copy(0, 0).start()

    locals_in.start()
    for j in (1, 0):
        own_local[j].wait()
        for b in range(lt):
            for k in range(3):
                at = (j, (t * lt + b) * 3 + k)
                wbuf[at] = wbuf[at] * pattern_ref[k, j, b].astype(F32)

    zero_halo = jnp.zeros((rows, tr), F32)
    for missing, place in ((t == 0, left_halo), (t == ranks - 1, right_halo)):
        @pl.when(missing)
        def _(place=place):
            odd[:, place] = zero_halo

            @pl.when(has_next)
            def _():
                nxt[:, place] = zero_halo

    @pl.when(p == parts - 1)
    def _():
        nxt[...] = jnp.zeros_like(nxt)

    for ref in (m_high, m_low):
        ref[pl.ds(0, tr), :] = jnp.zeros((tr, width), BF16)
        ref[pl.ds(tr + rows, tr), :] = jnp.zeros((tr, width), BF16)
    for j in (0, 1):
        @pl.when(has_left)
        def _(j=j):
            wbuf[j, 0] = jnp.zeros((tr, tr), F32)

        @pl.when(has_right)
        def _(j=j):
            wbuf[j, tiles * 3 - 1] = jnp.zeros((tr, tr), F32)

    for ref in (wc_high, wc_low, wt_high, wt_low):
        ref[...] = jnp.zeros_like(ref)
    start_own(1)
    start_own(0)

    chunk = 256

    def column_product(field, j):
        for i in range(lt // g):
            for c in range(g):
                for k in range(3):
                    high, low = split(wbuf[j, (t * lt + i * g + c) * 3 + k])
                    at = (i, pl.ds((c + k) * tr, tr), pl.ds(c * tr, tr))
                    wc_high[at] = high
                    wc_low[at] = low

        @pl.loop(0, rows // chunk)
        def _(r):
            start = pl.multiple_of(r * chunk, chunk)
            for i in range(lt // g):
                high, low = split(field[pl.ds(start, chunk), pl.ds(i * g * tr, span)])
                value = split_dot(high, low, wc_high[i], wc_low[i])
                at = (pl.ds(pl.multiple_of(start + tr, tr), chunk), pl.ds(i * g * tr, g * tr))
                high, low = split(value)
                m_high[at] = high
                m_low[at] = low

    def left_rows(j, owner, target, columns):
        @pl.loop(0, lt // g)
        def _(i):
            first = owner * lt + i * g
            for c in range(g):
                for k in range(3):
                    high, low = split(wbuf[j, (first + c) * 3 + k].T)
                    at = (pl.ds(c * tr, tr), pl.ds((c + k) * tr, tr))
                    wt_high[at] = high
                    wt_low[at] = low
            start = pl.multiple_of(first * tr, tr)
            source = pl.ds(start, span)
            value = split_dot(wt_high[...], wt_low[...], m_high[source, :], m_low[source, :])
            place = pl.ds(start, g * tr)
            target[place, columns] = loc[j, place, :].astype(F32) + value

    def left_round(j, k, target, columns):
        for d in (1, 0):
            @pl.when(comes(d, k))
            def _(d=d):
                left_rows(j, t - k if d == 0 else t + k, target, columns)

    def diagonal(index, field, offset):
        eye = lax.broadcasted_iota(jnp.int32, (tr, tr), 0) == lax.broadcasted_iota(jnp.int32, (tr, tr), 1)
        for c in range(lt):
            tile = field[pl.ds(pl.multiple_of(t * width + c * tr, tr), tr), pl.ds(offset + c * tr, tr)]
            var_ref[pl.ds(index, 1), pl.ds(c * tr, tr)] = jnp.sum(jnp.where(eye, tile, 0.0), axis=0, keepdims=True)

    receive(1, 1)

    @pl.when(has_next)
    def _():
        seed_copy(0, 0).wait_recv()

    blocks_but(t, has_next & has_left, lambda u: seed_copy(1, u).wait_recv())
    blocks_but(t, has_next & has_right, lambda u: seed_copy(2, u).wait_recv())
    mirror(nxt)
    column_product(nxt, 1)
    locals_in.wait()
    left_rows(1, t, odd, inner)
    left_round(1, 1, odd, inner)

    @pl.loop(2, ranks)
    def _(k):
        receive(1, k)
        left_round(1, k, odd, inner)

    diagonal(1, odd, tr)
    mirror(odd)
    blocks_but(t - 1, has_left, lambda u: halo_copy(1, u).start())
    blocks_but(t + 1, has_right, lambda u: halo_copy(0, u).start())

    @pl.loop(1, ranks - 1)
    def _(k):
        receive(0, k)

    blocks_but(t, has_left, lambda u: halo_copy(0, u).wait_recv())
    blocks_but(t, has_right, lambda u: halo_copy(1, u).wait_recv())
    column_product(odd, 0)
    everything = pl.ds(0, width)
    left_rows(0, t, out_ref, everything)

    @pl.loop(1, ranks - 1)
    def _(k):
        left_round(0, k, out_ref, everything)

    receive(0, ranks - 1)
    left_round(0, ranks - 1, out_ref, everything)
    diagonal(0, out_ref, 0)

    for j in (1, 0):
        for d in (1, 0):
            @pl.when(toward(d)[1])
            def _(j=j, d=d):
                with_w(j, d, 0, False, lambda copy: copy.wait_send())

                @pl.loop(1, ranks - 1)
                def _(k):
                    @pl.when(comes(d, k))
                    def _():
                        with_w(j, d, k, False, lambda copy: copy.wait_send())
    @pl.when(p > 0)
    def _():
        seed_copy(0, 0).wait_send()

    blocks_but(t + 1, (p > 0) & has_right, lambda u: seed_copy(1, u).wait_send())
    blocks_but(t - 1, (p > 0) & has_left, lambda u: seed_copy(2, u).wait_send())
    blocks_but(t + 1, has_right, lambda u: halo_copy(0, u).wait_send())
    blocks_but(t - 1, has_left, lambda u: halo_copy(1, u).wait_send())


def per_device(parts, ranks, local_inv, seed_inv, band, pattern):
    rows, width = seed_inv.shape[1:]
    lt, tr = band.shape[1], band.shape[3]
    tiles = rows // tr
    g = 2 if lt % 2 == 0 else 1
    span = (g + 2) * tr
    dma = pltpu.SemaphoreType.DMA
    out, var = pl.pallas_call(
        functools.partial(kernel, parts, ranks),
        out_shape=(pltpu.VMEM((rows, width), F32), pltpu.VMEM((2, width), F32)),
        in_specs=[pl.BlockSpec(memory_space=pltpu.HBM)] * 3 + [pl.BlockSpec(memory_space=pltpu.SMEM)],
        out_specs=(pl.BlockSpec(memory_space=pltpu.VMEM), pl.BlockSpec(memory_space=pltpu.VMEM)),
        scratch_shapes=[
            pltpu.VMEM((rows, width + 2 * tr), F32),
            pltpu.VMEM((rows, width + 2 * tr), F32),
            pltpu.VMEM((2, tiles * 3, tr, tr), F32),
            pltpu.VMEM((rows + 2 * tr, width), BF16),
            pltpu.VMEM((rows + 2 * tr, width), BF16),
            pltpu.VMEM((2, rows, width), BF16),
            pltpu.VMEM((lt // g, span, g * tr), BF16),
            pltpu.VMEM((lt // g, span, g * tr), BF16),
            pltpu.VMEM((g * tr, span), BF16),
            pltpu.VMEM((g * tr, span), BF16),
            dma((2, 2, ranks + 1)),
            dma((2, 2, ranks + 1)),
            dma((3, ranks)),
            dma((3, ranks)),
            dma((2, ranks)),
            dma((2, ranks)),
            dma((3,)),
        ],
        compiler_params=pltpu.CompilerParams(
            collective_id=0, has_side_effects=True, vmem_limit_bytes=58 * 1024 * 1024
        ),
    )(local_inv, seed_inv, band.reshape(2, lt * 3, tr, tr), pattern.transpose(2, 0, 1))
    return out[None], var


def solution(mesh):
    placed = (
        P("tm", None, "tile"),
        P("tm", None, "tile"),
        P("tm", "tile", None, None, None),
        P("tm", "tile", None),
    )
    return jax.shard_map(
        functools.partial(per_device, mesh.shape["tm"], mesh.shape["tile"]),
        mesh=mesh,
        in_specs=placed,
        out_specs=(P("tm", None, "tile"), P("tm", "tile")),
        check_vma=False,
    )
```

```python
import functools

import jax
import jax.numpy as jnp
from jax import lax
from jax.experimental import pallas as pl
from jax.experimental.pallas import tpu as pltpu
from jax.sharding import PartitionSpec as P

F32 = jnp.float32
BF16 = jnp.bfloat16
MESH = pl.DeviceIdType.MESH


def split(value):
    high = value.astype(BF16)
    return high, (value - high.astype(F32)).astype(BF16)


def dot(a, b):
    return lax.dot_general(a, b, (((1,), (0,)), ((), ())), preferred_element_type=F32)


def split_dot(a_high, a_low, b_high, b_low):
    return dot(a_high, b_high) + (dot(a_high, b_low) + dot(a_low, b_high))


def kernel(parts, ranks, local_ref, seed_ref, band_ref, pattern_ref, out_ref, var_ref,
           nxt, odd, wbuf, m_high, m_low, loc, wc_high, wc_low, wt_high, wt_low,
           wsend, wrecv, nsend, nrecv, hsend, hrecv, lsem):
    p, t = lax.axis_index("tm"), lax.axis_index("tile")
    rows, width = seed_ref.shape[1], seed_ref.shape[2]
    tiles, tr = wbuf.shape[1] // 3, wbuf.shape[3]
    lt = width // tr
    g = 2 if lt % 2 == 0 else 1
    span = (g + 2) * tr
    inner = pl.ds(tr, width)
    left_halo, right_halo = pl.ds(0, tr), pl.ds(tr + width, tr)
    has_right, has_left = t < ranks - 1, t > 0
    has_next = p < parts - 1

    barrier = pltpu.get_barrier_semaphore()
    around = [(a, b) for a in (-1, 0, 1) for b in (-1, 0, 1) if (a, b) != (0, 0)]

    def present(a, b):
        return (p + a >= 0) & (p + a < parts) & (t + b >= 0) & (t + b < ranks)

    for a, b in around:
        @pl.when(present(a, b))
        def _(a=a, b=b):
            pl.semaphore_signal(barrier, inc=1, device_id={"tm": p + a, "tile": t + b}, device_id_type=MESH)
    near_tm = 1 + jnp.where(p > 0, 1, 0) + jnp.where(p < parts - 1, 1, 0)
    near_tile = 1 + jnp.where(t > 0, 1, 0) + jnp.where(t < ranks - 1, 1, 0)
    pl.semaphore_wait(barrier, near_tm * near_tile - 1)

    def toward(d):
        return (1, has_right) if d == 0 else (-1, has_left)

    def with_w(j, d, k, incoming, action):
        step, _ = toward(d)
        owner = t - step * k
        at_end = owner == (0 if d == 0 else ranks - 1)
        for condition, skip in ((at_end, 1), (jnp.logical_not(at_end), 0)):
            @pl.when(condition)
            def _(skip=skip):
                part = wbuf.at[j, pl.ds(owner * lt * 3 + (skip if d == 0 else 0), lt * 3 - skip)]
                action(pltpu.make_async_remote_copy(
                    src_ref=part, dst_ref=part,
                    send_sem=wsend.at[j, d, k], recv_sem=wrecv.at[j, d, k if incoming else k + 1],
                    device_id={"tile": t - step if incoming else t + step}, device_id_type=MESH))

    def comes(d, k):
        return t - k >= 0 if d == 0 else t + k < ranks

    def start_own(j):
        for d in (1, 0):
            @pl.when(toward(d)[1])
            def _(d=d):
                with_w(j, d, 0, False, lambda copy: copy.start())

    def receive(j, k):
        for d in (1, 0):
            @pl.when(comes(d, k))
            def _(d=d):
                with_w(j, d, k, True, lambda copy: copy.wait_recv())

                @pl.when(toward(d)[1])
                def _():
                    with_w(j, d, k, False, lambda copy: copy.start())

    def block(u):
        return pl.ds(u * width, width)

    def seed_copy(index, u):
        if index == 0:
            src, dst, target = seed_ref.at[0], nxt.at[:, inner], t
        elif index == 1:
            src, dst, target = seed_ref.at[0, block(u), pl.ds(width - tr, tr)], nxt.at[block(u), left_halo], t + 1
        else:
            src, dst, target = seed_ref.at[0, block(u), pl.ds(0, tr)], nxt.at[block(u), right_halo], t - 1
        return pltpu.make_async_remote_copy(
            src_ref=src, dst_ref=dst, send_sem=nsend.at[index, u], recv_sem=nrecv.at[index, u],
            device_id={"tm": p - 1, "tile": target}, device_id_type=MESH)

    def halo_copy(d, u):
        if d == 0:
            src, dst, target = odd.at[block(u), pl.ds(width, tr)], odd.at[block(u), left_halo], t + 1
        else:
            src, dst, target = odd.at[block(u), pl.ds(tr, tr)], odd.at[block(u), right_halo], t - 1
        return pltpu.make_async_remote_copy(
            src_ref=src, dst_ref=dst, send_sem=hsend.at[d, u], recv_sem=hrecv.at[d, u],
            device_id={"tile": target}, device_id_type=MESH)

    def blocks_but(skipped, does, action):
        @pl.loop(0, ranks)
        def _(u):
            @pl.when(does & (u != skipped))
            def _():
                action(u)

    def mirror(field):
        for does, row, place in ((has_left, t * width - tr, left_halo), (has_right, (t + 1) * width, right_halo)):
            @pl.when(does)
            def _(row=row, place=place):
                for i in range(lt):
                    tile = field[pl.ds(pl.multiple_of(row, tr), tr), pl.ds(tr + i * tr, tr)]
                    field[pl.ds(pl.multiple_of(t * width + i * tr, tr), tr), place] = tile.T

    own_local = [pltpu.make_async_copy(band_ref.at[j], wbuf.at[j, pl.ds(t * lt * 3, lt * 3)], lsem.at[j]) for j in (0, 1)]
    locals_in = pltpu.make_async_copy(local_ref, loc, lsem.at[2])
    for copy in own_local[::-1]:
        copy.start()
    blocks_but(t + 1, (p > 0) & has_right, lambda u: seed_copy(1, u).start())
    blocks_but(t - 1, (p > 0) & has_left, lambda u: seed_copy(2, u).start())

    @pl.when(p > 0)
    def _():
        seed_copy(0, 0).start()

    locals_in.start()
    for j in (1, 0):
        own_local[j].wait()
        for b in range(lt):
            for k in range(3):
                at = (j, (t * lt + b) * 3 + k)
                wbuf[at] = wbuf[at] * pattern_ref[k, j, b].astype(F32)

    zero_halo = jnp.zeros((rows, tr), F32)
    for missing, place in ((t == 0, left_halo), (t == ranks - 1, right_halo)):
        @pl.when(missing)
        def _(place=place):
            odd[:, place] = zero_halo

            @pl.when(has_next)
            def _():
                nxt[:, place] = zero_halo

    @pl.when(p == parts - 1)
    def _():
        nxt[...] = jnp.zeros_like(nxt)

    for ref in (m_high, m_low):
        ref[pl.ds(0, tr), :] = jnp.zeros((tr, width), BF16)
        ref[pl.ds(tr + rows, tr), :] = jnp.zeros((tr, width), BF16)
    for j in (0, 1):
        @pl.when(has_left)
        def _(j=j):
            wbuf[j, 0] = jnp.zeros((tr, tr), F32)

        @pl.when(has_right)
        def _(j=j):
            wbuf[j, tiles * 3 - 1] = jnp.zeros((tr, tr), F32)

    for ref in (wc_high, wc_low, wt_high, wt_low):
        ref[...] = jnp.zeros_like(ref)
    start_own(1)
    start_own(0)

    chunk = 256

    def column_product(field, j):
        for i in range(lt // g):
            for c in range(g):
                for k in range(3):
                    high, low = split(wbuf[j, (t * lt + i * g + c) * 3 + k])
                    at = (i, pl.ds((c + k) * tr, tr), pl.ds(c * tr, tr))
                    wc_high[at] = high
                    wc_low[at] = low

        @pl.loop(0, rows // chunk)
        def _(r):
            start = pl.multiple_of(r * chunk, chunk)
            for i in range(lt // g):
                high, low = split(field[pl.ds(start, chunk), pl.ds(i * g * tr, span)])
                value = split_dot(high, low, wc_high[i], wc_low[i])
                at = (pl.ds(pl.multiple_of(start + tr, tr), chunk), pl.ds(i * g * tr, g * tr))
                high, low = split(value)
                m_high[at] = high
                m_low[at] = low

    def left_rows(j, owner, target, columns):
        @pl.loop(0, lt // g)
        def _(i):
            first = owner * lt + i * g
            for c in range(g):
                for k in range(3):
                    high, low = split(wbuf[j, (first + c) * 3 + k].T)
                    at = (pl.ds(c * tr, tr), pl.ds((c + k) * tr, tr))
                    wt_high[at] = high
                    wt_low[at] = low
            start = pl.multiple_of(first * tr, tr)
            source = pl.ds(start, span)
            value = split_dot(wt_high[...], wt_low[...], m_high[source, :], m_low[source, :])
            place = pl.ds(start, g * tr)
            target[place, columns] = loc[j, place, :].astype(F32) + value

    def left_round(j, k, target, columns):
        for d in (1, 0):
            @pl.when(comes(d, k))
            def _(d=d):
                left_rows(j, t - k if d == 0 else t + k, target, columns)

    def diagonal(index, field, offset):
        eye = lax.broadcasted_iota(jnp.int32, (tr, tr), 0) == lax.broadcasted_iota(jnp.int32, (tr, tr), 1)
        for c in range(lt):
            tile = field[pl.ds(pl.multiple_of(t * width + c * tr, tr), tr), pl.ds(offset + c * tr, tr)]
            var_ref[pl.ds(index, 1), pl.ds(c * tr, tr)] = jnp.sum(jnp.where(eye, tile, 0.0), axis=0, keepdims=True)

    receive(1, 1)
    receive(0, 1)

    @pl.when(has_next)
    def _():
        seed_copy(0, 0).wait_recv()

    blocks_but(t, has_next & has_left, lambda u: seed_copy(1, u).wait_recv())
    blocks_but(t, has_next & has_right, lambda u: seed_copy(2, u).wait_recv())
    mirror(nxt)
    column_product(nxt, 1)
    locals_in.wait()
    left_rows(1, t, odd, inner)
    left_round(1, 1, odd, inner)

    @pl.loop(2, ranks)
    def _(k):
        receive(1, k)
        left_round(1, k, odd, inner)

    diagonal(1, odd, tr)
    mirror(odd)
    blocks_but(t - 1, has_left, lambda u: halo_copy(1, u).start())
    blocks_but(t + 1, has_right, lambda u: halo_copy(0, u).start())

    @pl.loop(2, ranks - 1)
    def _(k):
        receive(0, k)

    blocks_but(t, has_left, lambda u: halo_copy(0, u).wait_recv())
    blocks_but(t, has_right, lambda u: halo_copy(1, u).wait_recv())
    column_product(odd, 0)
    everything = pl.ds(0, width)
    left_rows(0, t, out_ref, everything)

    @pl.loop(1, ranks - 1)
    def _(k):
        left_round(0, k, out_ref, everything)

    if ranks > 2:
        receive(0, ranks - 1)
    left_round(0, ranks - 1, out_ref, everything)
    diagonal(0, out_ref, 0)

    for j in (1, 0):
        for d in (1, 0):
            @pl.when(toward(d)[1])
            def _(j=j, d=d):
                with_w(j, d, 0, False, lambda copy: copy.wait_send())

                @pl.loop(1, ranks - 1)
                def _(k):
                    @pl.when(comes(d, k))
                    def _():
                        with_w(j, d, k, False, lambda copy: copy.wait_send())
    @pl.when(p > 0)
    def _():
        seed_copy(0, 0).wait_send()

    blocks_but(t + 1, (p > 0) & has_right, lambda u: seed_copy(1, u).wait_send())
    blocks_but(t - 1, (p > 0) & has_left, lambda u: seed_copy(2, u).wait_send())
    blocks_but(t + 1, has_right, lambda u: halo_copy(0, u).wait_send())
    blocks_but(t - 1, has_left, lambda u: halo_copy(1, u).wait_send())


def per_device(parts, ranks, local_inv, seed_inv, band, pattern):
    rows, width = seed_inv.shape[1:]
    lt, tr = band.shape[1], band.shape[3]
    tiles = rows // tr
    g = 2 if lt % 2 == 0 else 1
    span = (g + 2) * tr
    dma = pltpu.SemaphoreType.DMA
    out, var = pl.pallas_call(
        functools.partial(kernel, parts, ranks),
        out_shape=(pltpu.VMEM((rows, width), F32), pltpu.VMEM((2, width), F32)),
        in_specs=[pl.BlockSpec(memory_space=pltpu.HBM)] * 3 + [pl.BlockSpec(memory_space=pltpu.SMEM)],
        out_specs=(pl.BlockSpec(memory_space=pltpu.VMEM), pl.BlockSpec(memory_space=pltpu.VMEM)),
        scratch_shapes=[
            pltpu.VMEM((rows, width + 2 * tr), F32),
            pltpu.VMEM((rows, width + 2 * tr), F32),
            pltpu.VMEM((2, tiles * 3, tr, tr), F32),
            pltpu.VMEM((rows + 2 * tr, width), BF16),
            pltpu.VMEM((rows + 2 * tr, width), BF16),
            pltpu.VMEM((2, rows, width), BF16),
            pltpu.VMEM((lt // g, span, g * tr), BF16),
            pltpu.VMEM((lt // g, span, g * tr), BF16),
            pltpu.VMEM((g * tr, span), BF16),
            pltpu.VMEM((g * tr, span), BF16),
            dma((2, 2, ranks + 1)),
            dma((2, 2, ranks + 1)),
            dma((3, ranks)),
            dma((3, ranks)),
            dma((2, ranks)),
            dma((2, ranks)),
            dma((3,)),
        ],
        compiler_params=pltpu.CompilerParams(
            collective_id=0, has_side_effects=True, vmem_limit_bytes=58 * 1024 * 1024
        ),
    )(local_inv, seed_inv, band.reshape(2, lt * 3, tr, tr), pattern.transpose(2, 0, 1))
    return out[None], var


def solution(mesh):
    placed = (
        P("tm", None, "tile"),
        P("tm", None, "tile"),
        P("tm", "tile", None, None, None),
        P("tm", "tile", None),
    )
    return jax.shard_map(
        functools.partial(per_device, mesh.shape["tm"], mesh.shape["tile"]),
        mesh=mesh,
        in_specs=placed,
        out_specs=(P("tm", None, "tile"), P("tm", "tile")),
        check_vma=False,
    )
```
